32 devices in a mesh: groups: 2 (over x), lines: 16 (over z, y, core).
Axes of the slice: x: 2, y: 2, z: 4, core: 2. Of those that a mesh axis runs over, the one named last changes fastest.
Arguments:
- raw_echo: bfloat16 [8, 2, 2048, 512], P('groups', None, 'lines'), parts along dimension 0, may hold values from -6 to 6
- range_filter: bfloat16 [2, 512, 512], replicated, may hold values from -0.1875 to 0.1875
- azimuth_phase: float32 [512, 2048], P('lines'), may hold values from -3.140625 to 3.140625
- pair_offset: int32 [4], replicated, may hold values from 1 to 3
Outputs:
- filtered: float32 [8, 2, 128, 1024], P('groups', None, None, 'lines'), parts along dimension 0
The draws below stay inside these ranges and needn't reach their ends.
There are 2 independent parts, one for each index of `groups`. The reference program is written for one: setup_inputs(seed, part) draws one part's arguments, and reference() takes and returns one part's arrays. A program takes and returns all parts, laid end to end along the dimension named above; an argument that names none is the same for every part. Nothing has to cross between parts.
Inputs may be any that keep to these rules, and one draw needn't show every extreme that they name: Date d is paired with date (d + pair_offset[d]) mod 4.
All inputs are finite; a program needn't handle non-finite values.
Results may differ from the reference program's by a relative error of at most 0.0095.
Values may be sent and summed in bfloat16 or wider, within the bound.
A program may use at most 192 MiB of HBM per device.

```python
import jax
import jax.numpy as jnp
from jax import lax

DATES = 4
GATES = 512
ML_RG = 4
ML_AZ = 2
PATCH = 32
LINES = 2048


def touch_ends(drawn, own_key, low, largest):
    longest = drawn.shape.index(max(drawn.shape))
    spots = []
    for shift in (0, 1):
        where = [jax.random.randint(jax.random.fold_in(own_key, axis), (), 0, length) for axis, length in enumerate(drawn.shape)]
        where[longest] = (where[longest] + shift) % drawn.shape[longest]
        spots.append(tuple(where))
    return drawn.at[spots[0]].set(low).at[spots[1]].set(largest)


def steps_of(stream_key, shape, cuts, low, top_value):
    def one(dim, blocks):
        steps = jax.random.uniform(jax.random.fold_in(jax.random.fold_in(stream_key, 6), dim), (blocks,), jnp.float32, low / len(cuts), top_value / len(cuts))
        return jnp.repeat(jnp.exp(steps), shape[dim] // blocks).reshape((-1,) + (1,) * (len(shape) - dim - 1))

    factor_of = one(*cuts[0])
    for cut in cuts[1:]:
        factor_of = factor_of * one(*cut)
    return factor_of


def scatter_about(key, extent, width, bound, split=(), held_as=jnp.bfloat16):
    loudness = steps_of(key, extent, split, -0.22, 0.18) if split else 1.0
    values = jax.random.normal(key, extent, jnp.float32) * width * loudness
    return jnp.minimum(jnp.maximum(values, -bound), bound).astype(held_as)


def setup_inputs(seed: int = 0, part: int = 0) -> dict:
    key_list = jax.random.split(jax.random.key(seed), 5)
    own_keys = jax.random.split(jax.random.fold_in(key_list[4], part), 5)
    return {
        "raw_echo": scatter_about(own_keys[0], (DATES, 2, LINES, GATES), 1.0, 6.0, ((2, 16),)),
        "range_filter": scatter_about(key_list[1], (2, GATES, GATES), (2 * GATES) ** -0.5, 0.1875),
        "azimuth_phase": jnp.clip(jax.random.uniform(key_list[2], (GATES, LINES), jnp.float32, -3.140625, 3.140625), -3.140625, 3.140625),
        "pair_offset": touch_ends(jax.random.randint(key_list[3], (DATES,), 1, DATES), jax.random.fold_in(key_list[3], 1), 1, DATES - 1).astype(jnp.int32),
    }


PRECISION_MAX = lax.Precision.HIGHEST
BOX_FLOOR = 0.25

def compress(raw_echo, range_filter):
    w_real = jnp.stack([range_filter[0], -range_filter[1]])
    w_imag = jnp.stack([range_filter[1], range_filter[0]])
    stacked = jnp.stack([w_real, w_imag]).astype(jnp.float32)
    result = jnp.einsum('ecog,dclg->deol', stacked, raw_echo.astype(jnp.float32), precision=PRECISION_MAX)
    return result.astype(jnp.bfloat16)

def focus(compressed, azimuth_phase):
    signal = lax.complex(compressed[:, 0].astype(jnp.float32), compressed[:, 1].astype(jnp.float32))
    spectrum = jnp.fft.fft(signal, axis=-1)
    doppler = lax.complex(jnp.cos(azimuth_phase), jnp.sin(azimuth_phase))
    image = jnp.fft.ifft(spectrum * doppler, axis=-1)
    return jnp.stack([jnp.real(image), jnp.imag(image)], axis=1).astype(jnp.bfloat16)

def interfere(focused, pair_offset):
    date_count = focused.shape[0]
    partner_index = (jnp.arange(date_count, dtype=jnp.int32) + pair_offset) % date_count
    current = focused.astype(jnp.float32)
    partner = jnp.take(current, partner_index, axis=0)
    real_part = current[:, 0] * partner[:, 0] + current[:, 1] * partner[:, 1]
    imag_part = current[:, 1] * partner[:, 0] - current[:, 0] * partner[:, 1]
    joined = jnp.stack([real_part, imag_part], axis=1)
    shape_all = joined.shape
    joined = joined.reshape(shape_all[0], 2, shape_all[2] // ML_RG, ML_RG, shape_all[3] // ML_AZ, ML_AZ)
    return lax.optimization_barrier(jnp.mean(joined, axis=(3, 5)))

def tri_window(patch_len):
    position = jnp.arange(patch_len, dtype=jnp.float32)
    return 1.0 - jnp.abs(position - (patch_len - 1) / 2.0) / (patch_len // 2)

def filter_patches(block_real, block_imag):
    spectra = jnp.fft.fft2(lax.complex(block_real, block_imag), axes=(2, 4))
    spectral = jnp.real(spectra) ** 2 + jnp.imag(spectra) ** 2
    smooth = jnp.zeros_like(spectral)
    for shift_gate in (-1, 0, 1):
        for shift_line in (-1, 0, 1):
            smooth = smooth + jnp.roll(spectral, (shift_gate, shift_line), axis=(2, 4))
    smooth = smooth / 9.0
    level_mean = lax.optimization_barrier(jnp.mean(smooth, axis=(2, 4), keepdims=True)) + 1e-06
    weight = jnp.sqrt(smooth / level_mean + BOX_FLOOR)
    inverse = jnp.fft.ifft2(spectra * weight, axes=(2, 4))
    window = tri_window(PATCH)
    window_two = window[:, None, None] * window[None, None, :]
    return (jnp.real(inverse) * window_two, jnp.imag(inverse) * window_two)

def goldstein(pad_real, pad_imag, gate_rows, line_cols):
    half_patch = PATCH // 2
    date_count = pad_real.shape[0]
    out_real = jnp.zeros((date_count, gate_rows, line_cols), jnp.float32)
    out_imag = jnp.zeros((date_count, gate_rows, line_cols), jnp.float32)
    for gate_odd in (0, 1):
        gate_start = gate_odd * half_patch
        gate_len = gate_rows + PATCH - 2 * gate_odd * half_patch
        gate_crop = half_patch - gate_start
        for line_odd in (0, 1):
            line_start = line_odd * half_patch
            line_len = line_cols + PATCH - 2 * line_odd * half_patch
            line_crop = half_patch - line_start
            shape_new = (date_count, gate_len // PATCH, PATCH, line_len // PATCH, PATCH)
            block_real = pad_real[:, gate_start:gate_start + gate_len, line_start:line_start + line_len].reshape(shape_new)
            block_imag = pad_imag[:, gate_start:gate_start + gate_len, line_start:line_start + line_len].reshape(shape_new)
            part_real, part_imag = filter_patches(block_real, block_imag)
            part_real = part_real.reshape(date_count, gate_len, line_len)
            part_imag = part_imag.reshape(date_count, gate_len, line_len)
            out_real = out_real + part_real[:, gate_crop:gate_crop + gate_rows, line_crop:line_crop + line_cols]
            out_imag = out_imag + part_imag[:, gate_crop:gate_crop + gate_rows, line_crop:line_crop + line_cols]
    return (out_real, out_imag)

def reference(raw_echo, range_filter, azimuth_phase, pair_offset):
    compressed = compress(raw_echo, range_filter)
    focused = focus(compressed, azimuth_phase)
    looks = interfere(focused, pair_offset)
    half_patch = PATCH // 2
    padded = jnp.pad(looks, ((0, 0), (0, 0), (half_patch, half_patch), (half_patch, half_patch)))
    out_real, out_imag = goldstein(padded[:, 0], padded[:, 1], looks.shape[2], looks.shape[3])
    return jnp.stack([out_real, out_imag], axis=1)
```

```python
import functools

import jax
import jax.numpy as jnp
import ml_dtypes
import numpy as np
from jax import lax
from jax.experimental import pallas as pl
from jax.experimental.pallas import tpu as pltpu
from jax.sharding import PartitionSpec as P

ML_RG = 4
ML_AZ = 2
PATCH = 32
HALF = PATCH // 2
BOX_FLOOR = 0.25
LANES = 128
VMEM = pl.BlockSpec(memory_space=pltpu.VMEM)


def split_table(table):
    high = table.astype(np.float32).astype(ml_dtypes.bfloat16)
    low = (table - high.astype(np.float64)).astype(np.float32).astype(ml_dtypes.bfloat16)
    return np.stack([high, low])


def right_block(table):
    return np.block([[table.real, table.imag], [-table.imag, table.real]])


def left_block(table):
    return np.block([[table.real, -table.imag], [table.imag, table.real]])


def split(value):
    high = value.astype(jnp.bfloat16)
    low = (value - high.astype(jnp.float32)).astype(jnp.bfloat16)
    return high, low


def mm(a, b):
    return jnp.dot(a, b, preferred_element_type=jnp.float32)


def times_table(value, table):
    high, low = split(value)
    return mm(high, table[0]) + mm(low, table[0]) + mm(high, table[1])


def table_times(table, value):
    high, low = split(value)
    return mm(table[0], high) + mm(table[0], low) + mm(table[1], high)


def exact_times(value, table):
    high, low = split(value)
    return mm(high, table) + mm(low, table)


def times_exact(table, value):
    high, low = split(value)
    return mm(table, high) + mm(table, low)


def fft_leading(re, im, sign):
    count = len(re)
    if count == 1:
        return re, im
    if count == 2:
        return [re[0] + re[1], re[0] - re[1]], [im[0] + im[1], im[0] - im[1]]
    er, ei = fft_leading(re[0::2], im[0::2], sign)
    odr, odi = fft_leading(re[1::2], im[1::2], sign)
    half = count // 2
    out_r, out_i = [None] * count, [None] * count
    for k in range(half):
        angle = sign * 2.0 * np.pi * k / count
        c, s = float(np.cos(angle)), float(np.sin(angle))
        if k == 0:
            tr, ti = odr[k], odi[k]
        elif 4 * k == count:
            tr, ti = (-odi[k], odr[k]) if sign > 0 else (odi[k], -odr[k])
        else:
            tr = odr[k] * c - odi[k] * s
            ti = odr[k] * s + odi[k] * c
        out_r[k], out_i[k] = er[k] + tr, ei[k] + ti
        out_r[k + half], out_i[k + half] = er[k] - tr, ei[k] - ti
    return out_r, out_i


def compress_kernel(raw_ref, filt_ref, out_ref):
    shards = out_ref.shape[0]
    gates, line_count = filt_ref.shape[1], raw_ref.shape[2]
    weights = filt_ref[...].reshape(2 * gates, gates)
    contract = (((1,), (1,)), ((), ()))
    first = lax.dot_general(weights, raw_ref[0, 0], contract, preferred_element_type=jnp.float32)
    second = lax.dot_general(weights, raw_ref[0, 1], contract, preferred_element_type=jnp.float32)
    real = first[:gates] - second[gates:]
    imag = first[gates:] + second[:gates]
    shape = (shards, gates // shards, line_count)
    out_ref[:, 0, 0] = real.astype(jnp.bfloat16).reshape(shape)
    out_ref[:, 0, 1] = imag.astype(jnp.bfloat16).reshape(shape)


def compress(raw_echo, range_filter, shards):
    dates, _, line_count, gates = raw_echo.shape
    out = (shards, dates, 2, gates // shards, line_count)
    return pl.pallas_call(
        compress_kernel,
        grid=(dates,),
        in_specs=[
            pl.BlockSpec((1, 2, line_count, gates), lambda d: (d, 0, 0, 0)),
            pl.BlockSpec((2, gates, gates), lambda d: (0, 0, 0)),
        ],
        out_specs=pl.BlockSpec((shards, 1) + out[2:], lambda d: (0, d, 0, 0, 0)),
        out_shape=jax.ShapeDtypeStruct(out, jnp.bfloat16),
        name="compress",
    )(raw_echo, range_filter)


def focus_kernel(
    offset_ref, col_ref, cos_ref, sin_ref, twid_ref, fwd_ref, back_ref, gate_ref, main_ref, rim_ref,
    out_ref, work, focused,
):
    shards, _, _, gates, lanes = col_ref.shape
    dates = focused.shape[0]
    date = pl.program_id(0)
    chunk = min(gates, 8)
    rows = shards * gates
    for start in range(0, gates, chunk):
        part = pl.ds(start, chunk)
        re = [col_ref[s, 0, 0, part, :].astype(jnp.float32) for s in range(shards)]
        im = [col_ref[s, 0, 1, part, :].astype(jnp.float32) for s in range(shards)]
        re, im = fft_leading(re, im, -1.0)
        for k in range(shards):
            c, s = twid_ref[0, pl.ds(k, 1), :], twid_ref[1, pl.ds(k, 1), :]
            at = pl.ds(k * gates + start, chunk)
            work[at, :lanes] = re[k] * c + im[k] * s
            work[at, lanes:] = im[k] * c - re[k] * s
    spectrum = times_table(work[...], fwd_ref)
    c = cos_ref[...].reshape(rows, lanes)
    s = sin_ref[...].reshape(rows, lanes)
    re, im = spectrum[:, :lanes], spectrum[:, lanes:]
    shifted = jnp.concatenate([re * c - im * s, re * s + im * c], axis=1)
    work[...] = times_table(shifted, back_ref)
    for start in range(0, gates, chunk):
        re, im = [], []
        for k in range(shards):
            c, s = twid_ref[0, pl.ds(k, 1), :], twid_ref[1, pl.ds(k, 1), :]
            at = pl.ds(k * gates + start, chunk)
            a, b = work[at, :lanes], work[at, lanes:]
            re.append(a * c - b * s)
            im.append(b * c + a * s)
        re, im = fft_leading(re, im, 1.0)
        for n in range(shards):
            at = pl.ds(n * gates + start, chunk)
            focused[date, at, :lanes] = re[n].astype(jnp.bfloat16).astype(jnp.float32)
            focused[date, at, lanes:] = im[n].astype(jnp.bfloat16).astype(jnp.float32)

    @pl.when(date == dates - 1)
    def _():
        looks_rows = gate_ref.shape[0] // 3
        gate_looks = looks_rows // shards
        pieces = []
        rim = None
        for d in range(dates):
            partner = lax.rem(d + offset_ref[d], dates)
            a, b = focused[d, :, :lanes], focused[d, :, lanes:]
            p, q = focused[partner, :, :lanes], focused[partner, :, lanes:]
            joined = jnp.concatenate([a * p + b * q, b * p - a * q], axis=1)
            summed = times_exact(gate_ref[...], joined)
            pieces.append(exact_times(summed[:looks_rows], main_ref[...]))
            sides = jnp.concatenate([summed[looks_rows : 2 * looks_rows], summed[2 * looks_rows :]], axis=1)
            side = exact_times(sides, rim_ref[d % 2])
            if d % 2 == 0:
                rim = side
            else:
                pieces.append(rim + side)
        order = [pieces[i] for i in range(len(pieces)) if i % 3 != 2] + pieces[2::3]
        shaped = [piece.reshape(shards, gate_looks, lanes) for piece in order]
        out_ref[...] = jnp.concatenate(shaped, axis=1).astype(out_ref.dtype)


def focus_tables(shards, gates, lanes):
    total = shards * lanes
    k1, n2 = np.arange(shards), np.arange(lanes)
    angle = 2.0 * np.pi / total * (np.outer(k1, n2) % total)
    twiddle = np.stack([np.cos(angle), np.sin(angle)]).astype(np.float32)
    grid = np.exp(-2j * np.pi / lanes * (np.outer(n2, n2) % lanes))
    forward = split_table(right_block(grid))
    backward = split_table(right_block(np.conj(grid)) / total)
    group = np.kron(np.eye(gates // ML_RG), np.ones((1, ML_RG)))
    before = np.eye(shards, k=-1)
    after = np.eye(shards, k=1)
    gate_sum = np.concatenate([np.kron(m, group) for m in (np.eye(shards), before, after)])
    looks = lanes // ML_AZ
    pair = np.kron(np.eye(looks), np.ones((ML_AZ, 1))) / (ML_RG * ML_AZ)
    main = np.kron(np.eye(2), pair)
    rim = np.zeros((2, 4 * lanes, lanes))
    for parity in range(2):
        for part in range(2):
            low = parity * 4 * HALF + part * 2 * HALF
            source = part * lanes
            rim[parity, source : source + lanes, low : low + HALF] = pair[:, looks - HALF :]
            source += 2 * lanes
            rim[parity, source : source + lanes, low + HALF : low + 2 * HALF] = pair[:, :HALF]
    bf16 = ml_dtypes.bfloat16
    return twiddle, forward, backward, gate_sum.astype(bf16), main.astype(bf16), rim.astype(bf16)


def focus_looks(columns, cosine, sine, pair_offset):
    shards, dates, _, gates, lanes = columns.shape
    tables = focus_tables(shards, gates, lanes)
    rows = shards * gates
    slabs = dates + dates // 2
    whole = lambda array: pl.BlockSpec(array.shape, lambda d, *_: (0,) * array.ndim)
    out = (shards, slabs * (gates // ML_RG), lanes)
    return pl.pallas_call(
        focus_kernel,
        grid_spec=pltpu.PrefetchScalarGridSpec(
            num_scalar_prefetch=1,
            grid=(dates,),
            in_specs=[
                pl.BlockSpec((shards, 1, 2, gates, lanes), lambda d, *_: (0, d, 0, 0, 0)),
                whole(cosine),
                whole(sine),
            ]
            + [whole(table) for table in tables],
            out_specs=pl.BlockSpec(out, lambda d, *_: (0, 0, 0)),
            scratch_shapes=[
                pltpu.VMEM((rows, 2 * lanes), jnp.float32),
                pltpu.VMEM((dates, rows, 2 * lanes), jnp.float32),
            ],
        ),
        out_shape=jax.ShapeDtypeStruct(out, jnp.bfloat16),
        name="focus",
    )(pair_offset, columns, cosine, sine, *tables)


def tri_window():
    return 1.0 - np.abs(np.arange(PATCH) - (PATCH - 1) / 2.0) / HALF


def patch_maps(cells, starts):
    count = len(starts)
    forward = np.zeros((cells, count, PATCH), np.complex128)
    backward = np.zeros((count, PATCH, cells), np.complex128)
    window, k = tri_window(), np.arange(PATCH)
    for patch, start in enumerate(starts):
        for a in range(PATCH):
            cell = start + a
            if 0 <= cell < cells:
                wave = np.exp(2j * np.pi / PATCH * (k * a % PATCH))
                forward[cell, patch] = np.conj(wave)
                backward[patch, :, cell] = wave * window[a] / PATCH
    return forward.reshape(cells, -1), backward.reshape(-1, cells)


def filter_tables(gate_rows, looks):
    gate_starts = range(-HALF, gate_rows - HALF + 1, HALF)
    line_starts = range(0, looks + 1, HALF)
    gate_fwd, gate_back = patch_maps(gate_rows, gate_starts)
    line_fwd, _ = patch_maps(looks + PATCH, line_starts)
    _, line_back = patch_maps(looks, [start - HALF for start in line_starts])
    used = len(line_starts) * PATCH
    width = -(-used // LANES) * LANES
    line_fwd = np.pad(line_fwd, ((0, 0), (0, width - used)))
    line_back = np.pad(line_back, ((0, width - used), (0, 0)))
    block = right_block(line_fwd).reshape(2, looks + PATCH, 2 * width)
    enter = np.zeros((2, 4 * looks, 2 * width))
    for parity in range(2):
        for part in range(2):
            enter[parity, part * looks : (part + 1) * looks] = block[part, HALF : HALF + looks]
            low = 2 * looks + parity * 4 * HALF + part * 2 * HALF
            enter[parity, low : low + HALF] = block[part, :HALF]
            enter[parity, low + HALF : low + 2 * HALF] = block[part, HALF + looks :]
    enter = np.stack([split_table(table) for table in enter])
    gap = (np.arange(PATCH)[:, None] - np.arange(PATCH)[None, :]) % PATCH
    near = (gap <= 1) | (gap == PATCH - 1)
    bf16 = ml_dtypes.bfloat16
    near_gate = np.kron(np.eye(len(gate_starts)), near).astype(bf16)
    near_line = np.kron(np.eye(width // PATCH), near).astype(bf16)
    level = np.kron(np.eye(width // PATCH), np.ones((PATCH, PATCH)) / PATCH**2).astype(bf16)
    return (
        enter,
        split_table(left_block(gate_fwd.T)),
        near_gate,
        near_line,
        level,
        split_table(left_block(gate_back.T)),
        split_table(right_block(line_back)),
    )


def filter_kernel(
    looks_ref, enter_ref, gate_ref, near_gate_ref, near_line_ref, level_ref, gate_back_ref, line_back_ref,
    out_ref,
):
    shards, slab_rows, lanes = looks_ref.shape
    dates, _, gate_rows, looks = out_ref.shape
    gate_looks = gate_rows // shards
    received = looks_ref[...].astype(jnp.float32)

    def slab(index):
        return received[:, index * gate_looks : (index + 1) * gate_looks].reshape(gate_rows, lanes)

    for date in range(dates):
        cells = jnp.concatenate([slab(date), slab(dates + date // 2)], axis=1).astype(jnp.bfloat16)
        half = mm(cells, enter_ref[date % 2, 0]) + mm(cells, enter_ref[date % 2, 1])
        width = half.shape[1] // 2
        both = jnp.concatenate([half[:, :width], half[:, width:]], axis=0)
        spectra = table_times(gate_ref, both)
        rows = spectra.shape[0] // 2
        re, im = spectra[:rows], spectra[rows:]
        power = re * re + im * im
        near = mm(near_gate_ref[...], power.astype(jnp.bfloat16))
        near = mm(near.astype(jnp.bfloat16), near_line_ref[...])
        sums = jnp.sum(power.reshape(rows // PATCH, PATCH, width), axis=1)
        level = exact_times(sums, level_ref[...])
        scale = 1.0 / (9.0 * (level + 1e-06))
        near = near.reshape(rows // PATCH, PATCH, width) * scale[:, None, :]
        weight = jnp.sqrt(near + BOX_FLOOR).reshape(rows, width)
        weighted = jnp.concatenate([re * weight, im * weight], axis=0)
        image = table_times(gate_back_ref, weighted)
        image = jnp.concatenate([image[:gate_rows], image[gate_rows:]], axis=1)
        result = times_table(image, line_back_ref)
        out_ref[date, 0] = result[:, :looks]
        out_ref[date, 1] = result[:, looks:]


def filter_looks(received, dates, gate_rows, looks):
    tables = filter_tables(gate_rows, looks)
    return pl.pallas_call(
        filter_kernel,
        in_specs=[VMEM] * (1 + len(tables)),
        out_specs=VMEM,
        out_shape=jax.ShapeDtypeStruct((dates, 2, gate_rows, looks), jnp.float32),
        name="goldstein",
    )(received, *tables)


def exchange(blocks):
    return lax.all_to_all(blocks, "lines", split_axis=0, concat_axis=0, tiled=True)


def body(raw_echo, range_filter, azimuth_phase, pair_offset):
    shards = lax.axis_size("lines")
    dates, _, line_count, gates = raw_echo.shape
    gate_cols, line_total = azimuth_phase.shape
    columns = exchange(compress(raw_echo, range_filter, shards))
    phase = azimuth_phase.reshape(gate_cols, line_count, shards).transpose(2, 0, 1)
    looks = focus_looks(columns, jnp.cos(phase), jnp.sin(phase), pair_offset)
    return filter_looks(exchange(looks), dates, gates // ML_RG, line_count // ML_AZ)


def solution(mesh):
    placed = (P("groups", None, "lines", None), P(), P("lines", None), P())
    return jax.shard_map(
        body,
        mesh=mesh,
        in_specs=placed,
        out_specs=P("groups", None, None, "lines"),
        check_vma=False,
    )
```

```python
import functools

import jax
import jax.numpy as jnp
import ml_dtypes
import numpy as np
from jax import lax
from jax.experimental import pallas as pl
from jax.experimental.pallas import tpu as pltpu
from jax.sharding import PartitionSpec as P

ML_RG = 4
ML_AZ = 2
PATCH = 32
HALF = PATCH // 2
BOX_FLOOR = 0.25
LANES = 128
VMEM = pl.BlockSpec(memory_space=pltpu.VMEM)


def split_table(table):
    high = table.astype(np.float32).astype(ml_dtypes.bfloat16)
    low = (table - high.astype(np.float64)).astype(np.float32).astype(ml_dtypes.bfloat16)
    return np.stack([high, low])


def right_block(table):
    return np.block([[table.real, table.imag], [-table.imag, table.real]])


def left_block(table):
    return np.block([[table.real, -table.imag], [table.imag, table.real]])


def split(value):
    high = value.astype(jnp.bfloat16)
    low = (value - high.astype(jnp.float32)).astype(jnp.bfloat16)
    return high, low


def mm(a, b):
    return jnp.dot(a, b, preferred_element_type=jnp.float32)


def times_table(value, table):
    high, low = split(value)
    return mm(high, table[0]) + mm(low, table[0]) + mm(high, table[1])


def exact_times(value, table):
    high, low = split(value)
    return mm(high, table) + mm(low, table)


def times_exact(table, value):
    high, low = split(value)
    return mm(table, high) + mm(table, low)


def fft_leading(re, im, sign):
    count = len(re)
    if count == 1:
        return re, im
    if count == 2:
        return [re[0] + re[1], re[0] - re[1]], [im[0] + im[1], im[0] - im[1]]
    er, ei = fft_leading(re[0::2], im[0::2], sign)
    odr, odi = fft_leading(re[1::2], im[1::2], sign)
    half = count // 2
    out_r, out_i = [None] * count, [None] * count
    for k in range(half):
        angle = sign * 2.0 * np.pi * k / count
        c, s = float(np.cos(angle)), float(np.sin(angle))
        if k == 0:
            tr, ti = odr[k], odi[k]
        elif 4 * k == count:
            tr, ti = (-odi[k], odr[k]) if sign > 0 else (odi[k], -odr[k])
        else:
            tr = odr[k] * c - odi[k] * s
            ti = odr[k] * s + odi[k] * c
        out_r[k], out_i[k] = er[k] + tr, ei[k] + ti
        out_r[k + half], out_i[k + half] = er[k] - tr, ei[k] - ti
    return out_r, out_i


def stack_kernel(
    shards, offset_ref, raw_ref, filt_ref, phase_ref, twid_ref, fwd_ref, back_ref, gate_ref, main_ref, rim_ref,
    out_ref, sent, columns, trig, work, focused, looks_sent, looks_got, send_sem, recv_sem,
):
    dates, _, line_count, total_gates = raw_ref.shape
    gates, lanes = columns.shape[3], columns.shape[4]
    rows = shards * gates
    me = lax.axis_index("lines")

    def ring(step):
        return lax.rem(me + step, shards)

    barrier = pltpu.get_barrier_semaphore()

    @pl.loop(1, shards)
    def _(step):
        pl.semaphore_signal(barrier, inc=1, device_id={"lines": ring(step)}, device_id_type=pl.DeviceIdType.MESH)

    def compress(date):
        weights = filt_ref[...].reshape(2 * total_gates, total_gates)
        contract = (((1,), (1,)), ((), ()))
        first = lax.dot_general(weights, raw_ref[date, 0], contract, preferred_element_type=jnp.float32)
        second = lax.dot_general(weights, raw_ref[date, 1], contract, preferred_element_type=jnp.float32)
        real = first[:total_gates] - second[total_gates:]
        imag = first[total_gates:] + second[:total_gates]
        shape = (shards, gates, line_count)
        sent[date, :, 0] = real.astype(jnp.bfloat16).reshape(shape)
        sent[date, :, 1] = imag.astype(jnp.bfloat16).reshape(shape)

    def block(source, target, slot, peer):
        return pltpu.make_async_remote_copy(
            src_ref=source, dst_ref=target, send_sem=send_sem.at[slot], recv_sem=recv_sem.at[slot],
            device_id={"lines": peer}, device_id_type=pl.DeviceIdType.MESH,
        )

    def send_date(date):
        @pl.loop(1, shards)
        def _(step):
            peer = ring(step)
            block(sent.at[date, peer], columns.at[date, me], date, peer).start()

        columns[date, me] = sent[date, me]

    def arrived(date):
        part = pl.ds(0, shards - 1)
        return block(sent.at[date, part], columns.at[date, part], date, ring(1))

    compress(0)
    pl.semaphore_wait(barrier, shards - 1)
    send_date(0)

    @pl.loop(1, dates)
    def _(date):
        compress(date)
        send_date(date)

    trig[0] = jnp.cos(phase_ref[...].reshape(rows, lanes))
    trig[1] = jnp.sin(phase_ref[...].reshape(rows, lanes))
    chunk = min(gates, 8)

    @pl.loop(0, dates)
    def _(date):
        arrived(date).wait_recv()
        for start in range(0, gates, chunk):
            part = pl.ds(start, chunk)
            re = [columns[date, s, 0, part, :].astype(jnp.float32) for s in range(shards)]
            im = [columns[date, s, 1, part, :].astype(jnp.float32) for s in range(shards)]
            re, im = fft_leading(re, im, -1.0)
            for k in range(shards):
                c, s = twid_ref[0, pl.ds(k, 1), :], twid_ref[1, pl.ds(k, 1), :]
                at = pl.ds(k * gates + start, chunk)
                work[at, :lanes] = re[k] * c + im[k] * s
                work[at, lanes:] = im[k] * c - re[k] * s
        spectrum = times_table(work[...], fwd_ref)
        c, s = trig[0], trig[1]
        re, im = spectrum[:, :lanes], spectrum[:, lanes:]
        shifted = jnp.concatenate([re * c - im * s, re * s + im * c], axis=1)
        work[...] = times_table(shifted, back_ref)
        for start in range(0, gates, chunk):
            re, im = [], []
            for k in range(shards):
                c, s = twid_ref[0, pl.ds(k, 1), :], twid_ref[1, pl.ds(k, 1), :]
                at = pl.ds(k * gates + start, chunk)
                a, b = work[at, :lanes], work[at, lanes:]
                re.append(a * c - b * s)
                im.append(b * c + a * s)
            re, im = fft_leading(re, im, 1.0)
            for n in range(shards):
                at = pl.ds(n * gates + start, chunk)
                focused[date, at, :lanes] = re[n].astype(jnp.bfloat16).astype(jnp.float32)
                focused[date, at, lanes:] = im[n].astype(jnp.bfloat16).astype(jnp.float32)

    looks_rows = gate_ref.shape[0] // 3
    gate_looks = looks_rows // shards
    pieces, rims = [], []
    for d in range(dates):
        partner = lax.rem(d + offset_ref[d], dates)
        a, b = focused[d, :, :lanes], focused[d, :, lanes:]
        p, q = focused[partner, :, :lanes], focused[partner, :, lanes:]
        joined = jnp.concatenate([a * p + b * q, b * p - a * q], axis=1)
        summed = times_exact(gate_ref[...], joined)
        pieces.append(exact_times(summed[:looks_rows], main_ref[...]))
        sides = jnp.concatenate([summed[looks_rows : 2 * looks_rows], summed[2 * looks_rows :]], axis=1)
        side = exact_times(sides, rim_ref[d % 2])
        if d % 2 == 0:
            rims.append(side)
        else:
            rims[-1] = rims[-1] + side
    shaped = [piece.reshape(shards, gate_looks, lanes) for piece in pieces + rims]
    looks_sent[...] = jnp.concatenate(shaped, axis=1).astype(looks_sent.dtype)

    @pl.loop(1, shards)
    def _(step):
        peer = ring(step)
        block(looks_sent.at[peer], looks_got.at[me], dates, peer).start()

    looks_got[me] = looks_sent[me]

    @pl.loop(0, dates)
    def _(date):
        arrived(date).wait_send()

    part = pl.ds(0, shards - 1)
    last = block(looks_sent.at[part], looks_got.at[part], dates, ring(1))
    last.wait_send()
    last.wait_recv()
    out_ref[...] = looks_got[...]


def focus_tables(shards, gates, lanes):
    total = shards * lanes
    k1, n2 = np.arange(shards), np.arange(lanes)
    angle = 2.0 * np.pi / total * (np.outer(k1, n2) % total)
    twiddle = np.stack([np.cos(angle), np.sin(angle)]).astype(np.float32)
    grid = np.exp(-2j * np.pi / lanes * (np.outer(n2, n2) % lanes))
    forward = split_table(right_block(grid))
    backward = split_table(right_block(np.conj(grid)) / total)
    group = np.kron(np.eye(gates // ML_RG), np.ones((1, ML_RG)))
    before = np.eye(shards, k=-1)
    after = np.eye(shards, k=1)
    gate_sum = np.concatenate([np.kron(m, group) for m in (np.eye(shards), before, after)])
    looks = lanes // ML_AZ
    pair = np.kron(np.eye(looks), np.ones((ML_AZ, 1))) / (ML_RG * ML_AZ)
    main = np.kron(np.eye(2), pair)
    rim = np.zeros((2, 4 * lanes, lanes))
    for parity in range(2):
        for part in range(2):
            low = parity * 4 * HALF + part * 2 * HALF
            source = part * lanes
            rim[parity, source : source + lanes, low : low + HALF] = pair[:, looks - HALF :]
            source += 2 * lanes
            rim[parity, source : source + lanes, low + HALF : low + 2 * HALF] = pair[:, :HALF]
    bf16 = ml_dtypes.bfloat16
    return twiddle, forward, backward, gate_sum.astype(bf16), main.astype(bf16), rim.astype(bf16)


def exchanged_looks(raw_echo, range_filter, phase, pair_offset):
    dates, _, line_count, _ = raw_echo.shape
    shards, gates, lanes = phase.shape
    tables = focus_tables(shards, gates, lanes)
    rows = shards * gates
    slab_rows = (dates + dates // 2) * (gates // ML_RG)
    block = (shards, slab_rows, lanes)
    columns = (dates, shards, 2, gates, line_count)
    return pl.pallas_call(
        functools.partial(stack_kernel, shards),
        in_specs=[pl.BlockSpec(memory_space=pltpu.SMEM)] + [VMEM] * (3 + len(tables)),
        out_specs=VMEM,
        out_shape=jax.ShapeDtypeStruct(block, jnp.bfloat16),
        scratch_shapes=[
            pltpu.VMEM(columns, jnp.bfloat16),
            pltpu.VMEM(columns, jnp.bfloat16),
            pltpu.VMEM((2, rows, lanes), jnp.float32),
            pltpu.VMEM((rows, 2 * lanes), jnp.float32),
            pltpu.VMEM((dates, rows, 2 * lanes), jnp.float32),
            pltpu.VMEM(block, jnp.bfloat16),
            pltpu.VMEM(block, jnp.bfloat16),
            pltpu.SemaphoreType.DMA((dates + 1,)),
            pltpu.SemaphoreType.DMA((dates + 1,)),
        ],
        compiler_params=pltpu.CompilerParams(collective_id=0, has_side_effects=True),
        name="stack",
    )(pair_offset, raw_echo, range_filter, phase, *tables)


def tri_window():
    return 1.0 - np.abs(np.arange(PATCH) - (PATCH - 1) / 2.0) / HALF


def patch_maps(cells, starts):
    count = len(starts)
    forward = np.zeros((cells, count, PATCH), np.complex128)
    backward = np.zeros((count, PATCH, cells), np.complex128)
    window, k = tri_window(), np.arange(PATCH)
    for patch, start in enumerate(starts):
        for a in range(PATCH):
            cell = start + a
            if 0 <= cell < cells:
                wave = np.exp(2j * np.pi / PATCH * (k * a % PATCH))
                forward[cell, patch] = np.conj(wave)
                backward[patch, :, cell] = wave * window[a] / PATCH
    return forward.reshape(cells, -1), backward.reshape(-1, cells)


def filter_tables(gate_rows, looks):
    gate_starts = range(-HALF, gate_rows - HALF + 1, HALF)
    line_starts = range(0, looks + 1, HALF)
    gate_fwd, gate_back = patch_maps(gate_rows, gate_starts)
    line_fwd, _ = patch_maps(looks + PATCH, line_starts)
    _, line_back = patch_maps(looks, [start - HALF for start in line_starts])
    used = len(line_starts) * PATCH
    width = -(-used // LANES) * LANES
    line_fwd = np.pad(line_fwd, ((0, 0), (0, width - used)))
    line_back = np.pad(line_back, ((0, width - used), (0, 0)))
    block = right_block(line_fwd).reshape(2, looks + PATCH, 2 * width)
    enter = np.zeros((2, 4 * looks, 2 * width))
    for parity in range(2):
        for part in range(2):
            enter[parity, part * looks : (part + 1) * looks] = block[part, HALF : HALF + looks]
            low = 2 * looks + parity * 4 * HALF + part * 2 * HALF
            enter[parity, low : low + HALF] = block[part, :HALF]
            enter[parity, low + HALF : low + 2 * HALF] = block[part, HALF + looks :]
    gap = (np.arange(PATCH)[:, None] - np.arange(PATCH)[None, :]) % PATCH
    near = (gap <= 1) | (gap == PATCH - 1)
    bf16 = ml_dtypes.bfloat16
    near_gate = np.kron(np.eye(len(gate_starts)), near).astype(bf16)
    near_line = np.kron(np.eye(width // PATCH), near).astype(bf16)
    level = np.kron(np.eye(width // PATCH), np.ones((PATCH, PATCH)) / PATCH**2).astype(bf16)
    return (
        enter.astype(bf16),
        left_block(gate_fwd.T).astype(bf16),
        near_gate,
        near_line,
        level,
        left_block(gate_back.T).astype(bf16),
        right_block(line_back).T.astype(bf16),
    )


def filter_kernel(
    looks_ref, enter_ref, gate_ref, near_gate_ref, near_line_ref, level_ref, gate_back_ref, line_back_ref,
    out_ref,
):
    shards, slab_rows, lanes = looks_ref.shape
    dates, _, looks, gate_rows = out_ref.shape
    gate_looks = gate_rows // shards
    received = looks_ref[...].astype(jnp.float32)

    def slab(index):
        return received[:, index * gate_looks : (index + 1) * gate_looks].reshape(gate_rows, lanes)

    for date in range(dates):
        cells = jnp.concatenate([slab(date), slab(dates + date // 2)], axis=1).astype(jnp.bfloat16)
        half = mm(cells, enter_ref[date % 2]).astype(jnp.bfloat16)
        width = half.shape[1] // 2
        both = jnp.concatenate([half[:, :width], half[:, width:]], axis=0)
        spectra = mm(gate_ref[...], both)
        rows = spectra.shape[0] // 2
        re, im = spectra[:rows], spectra[rows:]
        power = re * re + im * im
        near = mm(near_gate_ref[...], power.astype(jnp.bfloat16))
        near = mm(near.astype(jnp.bfloat16), near_line_ref[...])
        sums = jnp.sum(power.reshape(rows // PATCH, PATCH, width), axis=1)
        level = exact_times(sums, level_ref[...])
        scale = 1.0 / (9.0 * (level + 1e-06))
        near = near.reshape(rows // PATCH, PATCH, width) * scale[:, None, :]
        weight = jnp.sqrt(near + BOX_FLOOR).reshape(rows, width)
        weighted = jnp.concatenate([re * weight, im * weight], axis=0).astype(jnp.bfloat16)
        image = mm(gate_back_ref[...], weighted).astype(jnp.bfloat16)
        image = jnp.concatenate([image[:gate_rows], image[gate_rows:]], axis=1)
        contract = (((1,), (1,)), ((), ()))
        result = lax.dot_general(line_back_ref[...], image, contract, preferred_element_type=jnp.float32)
        out_ref[date, 0] = result[:looks]
        out_ref[date, 1] = result[looks:]


def filter_looks(received, dates, gate_rows, looks):
    tables = filter_tables(gate_rows, looks)
    return pl.pallas_call(
        filter_kernel,
        in_specs=[VMEM] * (1 + len(tables)),
        out_specs=VMEM,
        out_shape=jax.ShapeDtypeStruct((dates, 2, looks, gate_rows), jnp.float32),
        name="goldstein",
    )(received, *tables)


def body(raw_echo, range_filter, azimuth_phase, pair_offset):
    shards = lax.axis_size("lines")
    dates, _, line_count, gates = raw_echo.shape
    gate_cols, line_total = azimuth_phase.shape
    phase = azimuth_phase.reshape(gate_cols, line_count, shards).transpose(2, 0, 1)
    received = exchanged_looks(raw_echo, range_filter, phase, pair_offset)
    image = filter_looks(received, dates, gates // ML_RG, line_count // ML_AZ)
    return image.transpose(0, 1, 3, 2)


def solution(mesh):
    placed = (P("groups", None, "lines", None), P(), P("lines", None), P())
    return jax.shard_map(
        body,
        mesh=mesh,
        in_specs=placed,
        out_specs=P("groups", None, None, "lines"),
        check_vma=False,
    )
```

```python
import functools

import jax
import jax.numpy as jnp
import ml_dtypes
import numpy as np
from jax import lax
from jax.experimental import pallas as pl
from jax.experimental.pallas import tpu as pltpu
from jax.sharding import PartitionSpec as P

ML_RG = 4
ML_AZ = 2
PATCH = 32
HALF = PATCH // 2
BOX_FLOOR = 0.25
LANES = 128
VMEM = pl.BlockSpec(memory_space=pltpu.VMEM)


def split_table(table):
    high = table.astype(np.float32).astype(ml_dtypes.bfloat16)
    low = (table - high.astype(np.float64)).astype(np.float32).astype(ml_dtypes.bfloat16)
    return np.stack([high, low])


def right_block(table):
    return np.block([[table.real, table.imag], [-table.imag, table.real]])


def left_block(table):
    return np.block([[table.real, -table.imag], [table.imag, table.real]])


def split(value):
    high = value.astype(jnp.bfloat16)
    low = (value - high.astype(jnp.float32)).astype(jnp.bfloat16)
    return high, low


def mm(a, b):
    return jnp.dot(a, b, preferred_element_type=jnp.float32)


def times_table(value, table):
    high, low = split(value)
    return mm(high, table[0]) + mm(low, table[0]) + mm(high, table[1])


def exact_times(value, table):
    high, low = split(value)
    return mm(high, table) + mm(low, table)


def fft_leading(re, im, sign):
    count = len(re)
    if count == 1:
        return re, im
    if count == 2:
        return [re[0] + re[1], re[0] - re[1]], [im[0] + im[1], im[0] - im[1]]
    er, ei = fft_leading(re[0::2], im[0::2], sign)
    odr, odi = fft_leading(re[1::2], im[1::2], sign)
    half = count // 2
    out_r, out_i = [None] * count, [None] * count
    for k in range(half):
        angle = sign * 2.0 * np.pi * k / count
        c, s = float(np.cos(angle)), float(np.sin(angle))
        if k == 0:
            tr, ti = odr[k], odi[k]
        elif 4 * k == count:
            tr, ti = (-odi[k], odr[k]) if sign > 0 else (odi[k], -odr[k])
        else:
            tr = odr[k] * c - odi[k] * s
            ti = odr[k] * s + odi[k] * c
        out_r[k], out_i[k] = er[k] + tr, ei[k] + ti
        out_r[k + half], out_i[k + half] = er[k] - tr, ei[k] - ti
    return out_r, out_i


def filter_date(
    cells, parity, date, enter_ref, gate_ref, near_gate_ref, near_line_ref, level_ref, gate_back_ref, line_back_ref,
    out_ref,
):
    _, _, looks, gate_rows = out_ref.shape
    half = mm(cells, enter_ref[parity]).astype(jnp.bfloat16)
    width = half.shape[1] // 2
    both = jnp.concatenate([half[:, :width], half[:, width:]], axis=0)
    spectra = mm(gate_ref[...], both)
    rows = spectra.shape[0] // 2
    re, im = spectra[:rows], spectra[rows:]
    power = re * re + im * im
    near = mm(near_gate_ref[...], power.astype(jnp.bfloat16))
    near = mm(near.astype(jnp.bfloat16), near_line_ref[...])
    sums = jnp.sum(power.reshape(rows // PATCH, PATCH, width), axis=1)
    level = exact_times(sums, level_ref[...])
    scale = 1.0 / (9.0 * (level + 1e-06))
    near = near.reshape(rows // PATCH, PATCH, width) * scale[:, None, :]
    weight = jnp.sqrt(near + BOX_FLOOR).reshape(rows, width)
    weighted = jnp.concatenate([re * weight, im * weight], axis=0).astype(jnp.bfloat16)
    image = mm(gate_back_ref[...], weighted).astype(jnp.bfloat16)
    image = jnp.concatenate([image[:gate_rows], image[gate_rows:]], axis=1)
    contract = (((1,), (1,)), ((), ()))
    result = lax.dot_general(line_back_ref[...], image, contract, preferred_element_type=jnp.float32)
    out_ref[date, 0] = result[:looks]
    out_ref[date, 1] = result[looks:]


def stack_kernel(
    shards, offset_ref, raw_ref, filt_ref, phase_ref, *refs,
):
    count = (len(refs) - 12) // 2
    stored, out_ref, tables = refs[:count], refs[count], refs[count + 1 : 2 * count + 1]
    (sent, columns, turned, trig, work, focused, looks_sent, looks_got,
     send_sem, recv_sem, table_sem) = refs[2 * count + 1 :]
    twid_ref, fwd_ref, back_ref, gate_ref, main_ref, rim_ref = tables[:6]
    loads = [pltpu.make_async_copy(stored[i], tables[i], table_sem.at[i]) for i in range(count)]
    for load in loads:
        load.start()
    dates, _, line_count, total_gates = raw_ref.shape
    gates, lanes = columns.shape[3], columns.shape[4]
    rows = shards * gates
    me = lax.axis_index("lines")

    def ring(step):
        away = lax.div(step, 2) * (1 - 2 * lax.rem(step, 2)) + shards // 2
        return lax.rem(me + away, shards)

    barrier = pltpu.get_barrier_semaphore()

    @pl.loop(1, shards)
    def _(step):
        pl.semaphore_signal(barrier, inc=1, device_id={"lines": ring(step)}, device_id_type=pl.DeviceIdType.MESH)

    def compress(date):
        weights = filt_ref[...].reshape(2 * total_gates, total_gates)
        contract = (((1,), (1,)), ((), ()))
        first = lax.dot_general(weights, raw_ref[date, 0], contract, preferred_element_type=jnp.float32)
        second = lax.dot_general(weights, raw_ref[date, 1], contract, preferred_element_type=jnp.float32)
        real = first[:total_gates] - second[total_gates:]
        imag = first[total_gates:] + second[:total_gates]
        shape = (shards, gates, line_count)
        sent[date, :, 0] = real.astype(jnp.bfloat16).reshape(shape)
        sent[date, :, 1] = imag.astype(jnp.bfloat16).reshape(shape)

    def block(source, target, slot, peer):
        return pltpu.make_async_remote_copy(
            src_ref=source, dst_ref=target, send_sem=send_sem.at[slot], recv_sem=recv_sem.at[slot],
            device_id={"lines": peer}, device_id_type=pl.DeviceIdType.MESH,
        )

    def send_date(date):
        @pl.loop(1, shards)
        def _(step):
            peer = ring(step)
            block(sent.at[date, peer], columns.at[date, me], date, peer).start()

        columns[date, me] = sent[date, me]

    def arrived(date):
        part = pl.ds(0, shards - 1)
        return block(sent.at[date, part], columns.at[date, part], date, ring(1))

    compress(0)
    pl.semaphore_wait(barrier, shards - 1)
    send_date(0)

    @pl.loop(1, dates)
    def _(date):
        compress(date)
        send_date(date)

    turned[...] = phase_ref[...].T

    @pl.loop(0, shards)
    def _(k):
        phase = turned[pl.ds(k, lanes, stride=shards), :].T
        at = pl.ds(pl.multiple_of(k * gates, gates), gates)
        trig[0, at, :] = jnp.cos(phase)
        trig[1, at, :] = jnp.sin(phase)

    for load in loads[:6]:
        load.wait()
    chunk = min(gates, 8)

    @pl.loop(0, dates)
    def _(date):
        arrived(date).wait_recv()
        for start in range(0, gates, chunk):
            part = pl.ds(start, chunk)
            re = [columns[date, s, 0, part, :].astype(jnp.float32) for s in range(shards)]
            im = [columns[date, s, 1, part, :].astype(jnp.float32) for s in range(shards)]
            re, im = fft_leading(re, im, -1.0)
            for k in range(shards):
                c, s = twid_ref[0, pl.ds(k, 1), :], twid_ref[1, pl.ds(k, 1), :]
                at = pl.ds(k * gates + start, chunk)
                work[at, :lanes] = re[k] * c + im[k] * s
                work[at, lanes:] = im[k] * c - re[k] * s
        spectrum = times_table(work[...], fwd_ref)
        c, s = trig[0], trig[1]
        re, im = spectrum[:, :lanes], spectrum[:, lanes:]
        shifted = jnp.concatenate([re * c - im * s, re * s + im * c], axis=1)
        work[...] = times_table(shifted, back_ref)
        for start in range(0, gates, chunk):
            re, im = [], []
            for k in range(shards):
                c, s = twid_ref[0, pl.ds(k, 1), :], twid_ref[1, pl.ds(k, 1), :]
                at = pl.ds(k * gates + start, chunk)
                a, b = work[at, :lanes], work[at, lanes:]
                re.append(a * c - b * s)
                im.append(b * c + a * s)
            re, im = fft_leading(re, im, 1.0)
            for n in range(shards):
                at = pl.ds(n * gates + start, chunk)
                focused[date, at, :lanes] = re[n].astype(jnp.bfloat16).astype(jnp.float32)
                focused[date, at, lanes:] = im[n].astype(jnp.bfloat16).astype(jnp.float32)

    looks_rows = gate_ref.shape[0] // 3
    gate_looks = looks_rows // shards

    def gathered(pair):
        part = pl.ds(0, shards - 1)
        return block(looks_sent.at[pair, part], looks_got.at[pair, part], dates + pair, ring(1))

    for pair in range(dates // 2):
        pieces, rim = [], None
        for d in (2 * pair, 2 * pair + 1):
            partner = lax.rem(d + offset_ref[d], dates)
            a, b = focused[d, :, :lanes], focused[d, :, lanes:]
            p, q = focused[partner, :, :lanes], focused[partner, :, lanes:]
            joined = jnp.concatenate([a * p + b * q, b * p - a * q], axis=1).astype(jnp.bfloat16)
            summed = mm(gate_ref[...], joined).astype(jnp.bfloat16)
            pieces.append(mm(summed[:looks_rows], main_ref[...]))
            sides = jnp.concatenate([summed[looks_rows : 2 * looks_rows], summed[2 * looks_rows :]], axis=1)
            side = mm(sides, rim_ref[d % 2])
            rim = side if rim is None else rim + side
        shaped = [piece.reshape(shards, gate_looks, lanes) for piece in pieces + [rim]]
        looks_sent[pair] = jnp.concatenate(shaped, axis=1).astype(looks_sent.dtype)

        @pl.loop(1, shards)
        def _(step):
            peer = ring(step)
            block(looks_sent.at[pair, peer], looks_got.at[pair, me], dates + pair, peer).start()

        looks_got[pair, me] = looks_sent[pair, me]

    for load in loads[6:]:
        load.wait()

    @pl.loop(0, dates)
    def _(date):
        arrived(date).wait_send()

    for pair in range(dates // 2):
        gathered(pair).wait_recv()
        received = looks_got[pair].astype(jnp.float32)

        def slab(index):
            return received[:, index * gate_looks : (index + 1) * gate_looks].reshape(shards * gate_looks, lanes)

        for parity in range(2):
            cells = jnp.concatenate([slab(parity), slab(2)], axis=1).astype(jnp.bfloat16)
            filter_date(cells, parity, 2 * pair + parity, *tables[6:], out_ref)

    for pair in range(dates // 2):
        gathered(pair).wait_send()


def focus_tables(shards, gates, lanes):
    total = shards * lanes
    k1, n2 = np.arange(shards), np.arange(lanes)
    angle = 2.0 * np.pi / total * (np.outer(k1, n2) % total)
    twiddle = np.stack([np.cos(angle), np.sin(angle)]).astype(np.float32)
    grid = np.exp(-2j * np.pi / lanes * (np.outer(n2, n2) % lanes))
    forward = split_table(right_block(grid))
    backward = split_table(right_block(np.conj(grid)) / total)
    group = np.kron(np.eye(gates // ML_RG), np.ones((1, ML_RG)))
    before = np.eye(shards, k=-1)
    after = np.eye(shards, k=1)
    gate_sum = np.concatenate([np.kron(m, group) for m in (np.eye(shards), before, after)])
    looks = lanes // ML_AZ
    pair = np.kron(np.eye(looks), np.ones((ML_AZ, 1))) / (ML_RG * ML_AZ)
    main = np.kron(np.eye(2), pair)
    rim = np.zeros((2, 4 * lanes, lanes))
    for parity in range(2):
        for part in range(2):
            low = parity * 4 * HALF + part * 2 * HALF
            source = part * lanes
            rim[parity, source : source + lanes, low : low + HALF] = pair[:, looks - HALF :]
            source += 2 * lanes
            rim[parity, source : source + lanes, low + HALF : low + 2 * HALF] = pair[:, :HALF]
    bf16 = ml_dtypes.bfloat16
    return twiddle, forward, backward, gate_sum.astype(bf16), main.astype(bf16), rim.astype(bf16)


def filtered_looks(raw_echo, range_filter, azimuth_phase, pair_offset, shards):
    dates, _, lanes, total_gates = raw_echo.shape
    gates = azimuth_phase.shape[0]
    tables = focus_tables(shards, gates, lanes) + filter_tables(total_gates // ML_RG, lanes // ML_AZ)
    rows = shards * gates
    pairs = dates // 2
    block = (pairs, shards, 3 * (gates // ML_RG), lanes)
    columns = (dates, shards, 2, gates, lanes)
    return pl.pallas_call(
        functools.partial(stack_kernel, shards),
        in_specs=[pl.BlockSpec(memory_space=pltpu.SMEM)]
        + [VMEM] * 3
        + [pl.BlockSpec(memory_space=pl.ANY)] * len(tables),
        out_specs=VMEM,
        out_shape=jax.ShapeDtypeStruct((dates, 2, lanes // ML_AZ, total_gates // ML_RG), jnp.float32),
        scratch_shapes=[pltpu.VMEM(table.shape, table.dtype) for table in tables]
        + [
            pltpu.VMEM(columns, jnp.bfloat16),
            pltpu.VMEM(columns, jnp.bfloat16),
            pltpu.VMEM(azimuth_phase.shape[::-1], jnp.float32),
            pltpu.VMEM((2, rows, lanes), jnp.float32),
            pltpu.VMEM((rows, 2 * lanes), jnp.float32),
            pltpu.VMEM((dates, rows, 2 * lanes), jnp.float32),
            pltpu.VMEM(block, jnp.bfloat16),
            pltpu.VMEM(block, jnp.bfloat16),
            pltpu.SemaphoreType.DMA((dates + pairs,)),
            pltpu.SemaphoreType.DMA((dates + pairs,)),
            pltpu.SemaphoreType.DMA((len(tables),)),
        ],
        compiler_params=pltpu.CompilerParams(collective_id=0, has_side_effects=True),
        name="stack",
    )(pair_offset, raw_echo, range_filter, azimuth_phase, *tables)


def tri_window():
    return 1.0 - np.abs(np.arange(PATCH) - (PATCH - 1) / 2.0) / HALF


def patch_maps(cells, starts):
    count = len(starts)
    forward = np.zeros((cells, count, PATCH), np.complex128)
    backward = np.zeros((count, PATCH, cells), np.complex128)
    window, k = tri_window(), np.arange(PATCH)
    for patch, start in enumerate(starts):
        for a in range(PATCH):
            cell = start + a
            if 0 <= cell < cells:
                wave = np.exp(2j * np.pi / PATCH * (k * a % PATCH))
                forward[cell, patch] = np.conj(wave)
                backward[patch, :, cell] = wave * window[a] / PATCH
    return forward.reshape(cells, -1), backward.reshape(-1, cells)


def filter_tables(gate_rows, looks):
    gate_starts = range(-HALF, gate_rows - HALF + 1, HALF)
    line_starts = range(0, looks + 1, HALF)
    gate_fwd, gate_back = patch_maps(gate_rows, gate_starts)
    line_fwd, _ = patch_maps(looks + PATCH, line_starts)
    _, line_back = patch_maps(looks, [start - HALF for start in line_starts])
    used = len(line_starts) * PATCH
    width = -(-used // LANES) * LANES
    line_fwd = np.pad(line_fwd, ((0, 0), (0, width - used)))
    line_back = np.pad(line_back, ((0, width - used), (0, 0)))
    block = right_block(line_fwd).reshape(2, looks + PATCH, 2 * width)
    enter = np.zeros((2, 4 * looks, 2 * width))
    for parity in range(2):
        for part in range(2):
            enter[parity, part * looks : (part + 1) * looks] = block[part, HALF : HALF + looks]
            low = 2 * looks + parity * 4 * HALF + part * 2 * HALF
            enter[parity, low : low + HALF] = block[part, :HALF]
            enter[parity, low + HALF : low + 2 * HALF] = block[part, HALF + looks :]
    gap = (np.arange(PATCH)[:, None] - np.arange(PATCH)[None, :]) % PATCH
    near = (gap <= 1) | (gap == PATCH - 1)
    bf16 = ml_dtypes.bfloat16
    near_gate = np.kron(np.eye(len(gate_starts)), near).astype(bf16)
    near_line = np.kron(np.eye(width // PATCH), near).astype(bf16)
    level = np.kron(np.eye(width // PATCH), np.ones((PATCH, PATCH)) / PATCH**2).astype(bf16)
    return (
        enter.astype(bf16),
        left_block(gate_fwd.T).astype(bf16),
        near_gate,
        near_line,
        level,
        left_block(gate_back.T).astype(bf16),
        right_block(line_back).T.astype(bf16),
    )


def body(raw_echo, range_filter, azimuth_phase, pair_offset):
    shards = lax.axis_size("lines")
    image = filtered_looks(raw_echo, range_filter, azimuth_phase, pair_offset, shards)
    return image.transpose(0, 1, 3, 2)


def solution(mesh):
    placed = (P("groups", None, "lines", None), P(), P("lines", None), P())
    return jax.shard_map(
        body,
        mesh=mesh,
        in_specs=placed,
        out_specs=P("groups", None, None, "lines"),
        check_vma=False,
    )
```

```python
import functools

import jax
import jax.numpy as jnp
import ml_dtypes
import numpy as np
from jax import lax
from jax.experimental import pallas as pl
from jax.experimental.pallas import tpu as pltpu
from jax.sharding import PartitionSpec as P

ML_RG = 4
ML_AZ = 2
PATCH = 32
HALF = PATCH // 2
BOX_FLOOR = 0.25
LANES = 128
VMEM = pl.BlockSpec(memory_space=pltpu.VMEM)


def right_block(table):
    return np.block([[table.real, table.imag], [-table.imag, table.real]])


def left_block(table):
    return np.block([[table.real, -table.imag], [table.imag, table.real]])


def split(value):
    high = value.astype(jnp.bfloat16)
    low = (value - high.astype(jnp.float32)).astype(jnp.bfloat16)
    return high, low


def mm(a, b):
    return jnp.dot(a, b, preferred_element_type=jnp.float32)


def exact_times(value, table):
    high, low = split(value)
    return mm(high, table) + mm(low, table)


def fft_leading(re, im, sign):
    count = len(re)
    if count == 1:
        return re, im
    if count == 2:
        return [re[0] + re[1], re[0] - re[1]], [im[0] + im[1], im[0] - im[1]]
    er, ei = fft_leading(re[0::2], im[0::2], sign)
    odr, odi = fft_leading(re[1::2], im[1::2], sign)
    half = count // 2
    out_r, out_i = [None] * count, [None] * count
    for k in range(half):
        angle = sign * 2.0 * np.pi * k / count
        c, s = float(np.cos(angle)), float(np.sin(angle))
        if k == 0:
            tr, ti = odr[k], odi[k]
        elif 4 * k == count:
            tr, ti = (-odi[k], odr[k]) if sign > 0 else (odi[k], -odr[k])
        else:
            tr = odr[k] * c - odi[k] * s
            ti = odr[k] * s + odi[k] * c
        out_r[k], out_i[k] = er[k] + tr, ei[k] + ti
        out_r[k + half], out_i[k + half] = er[k] - tr, ei[k] - ti
    return out_r, out_i


def filter_date(
    cells, parity, date, enter_ref, gate_ref, near_gate_ref, near_line_ref, level_ref, gate_back_ref, line_back_ref,
    out_ref,
):
    _, _, looks, gate_rows = out_ref.shape
    half = mm(cells, enter_ref[parity]).astype(jnp.bfloat16)
    width = half.shape[1] // 2
    both = jnp.concatenate([half[:, :width], half[:, width:]], axis=0)
    spectra = mm(gate_ref[...], both)
    rows = spectra.shape[0] // 2
    re, im = spectra[:rows], spectra[rows:]
    power = re * re + im * im
    near = mm(near_gate_ref[...], power.astype(jnp.bfloat16))
    near = mm(near.astype(jnp.bfloat16), near_line_ref[...])
    sums = jnp.sum(power.reshape(rows // PATCH, PATCH, width), axis=1)
    level = exact_times(sums, level_ref[...])
    scale = 1.0 / (9.0 * (level + 1e-06))
    near = near.reshape(rows // PATCH, PATCH, width) * scale[:, None, :]
    weight = jnp.sqrt(near + BOX_FLOOR).reshape(rows, width)
    weighted = jnp.concatenate([re * weight, im * weight], axis=0).astype(jnp.bfloat16)
    image = mm(gate_back_ref[...], weighted).astype(jnp.bfloat16)
    image = jnp.concatenate([image[:gate_rows], image[gate_rows:]], axis=1)
    contract = (((1,), (1,)), ((), ()))
    result = lax.dot_general(line_back_ref[...], image, contract, preferred_element_type=jnp.float32)
    out_ref[date, 0] = result[:looks]
    out_ref[date, 1] = result[looks:]


def stack_kernel(
    shards, offset_ref, raw_ref, filt_ref, phase_ref, *refs,
):
    count = (len(refs) - 12) // 2
    stored, out_ref, tables = refs[:count], refs[count], refs[count + 1 : 2 * count + 1]
    (sent, columns, turned, trig, work, focused, looks_sent, looks_got,
     send_sem, recv_sem, table_sem) = refs[2 * count + 1 :]
    twid_ref, fwd_ref, back_ref, gate_ref, main_ref, rim_ref = tables[:6]
    loads = [pltpu.make_async_copy(stored[i], tables[i], table_sem.at[i]) for i in range(count)]
    for load in loads:
        load.start()
    dates, _, line_count, total_gates = raw_ref.shape
    gates, lanes = columns.shape[3], columns.shape[4]
    rows = shards * gates
    me = lax.axis_index("lines")

    def ring(step):
        return lax.rem(me + step, shards)

    barrier = pltpu.get_barrier_semaphore()

    @pl.loop(1, shards)
    def _(step):
        pl.semaphore_signal(barrier, inc=1, device_id={"lines": ring(step)}, device_id_type=pl.DeviceIdType.MESH)

    def compress(date):
        weights = filt_ref[...].reshape(2 * total_gates, total_gates)
        contract = (((1,), (1,)), ((), ()))
        first = lax.dot_general(weights, raw_ref[date, 0], contract, preferred_element_type=jnp.float32)
        second = lax.dot_general(weights, raw_ref[date, 1], contract, preferred_element_type=jnp.float32)
        real = first[:total_gates] - second[total_gates:]
        imag = first[total_gates:] + second[:total_gates]
        shape = (shards, gates, line_count)
        sent[date, :, 0] = real.astype(jnp.bfloat16).reshape(shape)
        sent[date, :, 1] = imag.astype(jnp.bfloat16).reshape(shape)

    def block(source, target, slot, peer):
        return pltpu.make_async_remote_copy(
            src_ref=source, dst_ref=target, send_sem=send_sem.at[slot], recv_sem=recv_sem.at[slot],
            device_id={"lines": peer}, device_id_type=pl.DeviceIdType.MESH,
        )

    def send_date(date):
        @pl.loop(1, shards)
        def _(step):
            peer = ring(step)
            block(sent.at[date, peer], columns.at[date, me], date, peer).start()

        columns[date, me] = sent[date, me]

    def arrived(date):
        part = pl.ds(0, shards - 1)
        return block(sent.at[date, part], columns.at[date, part], date, ring(1))

    compress(0)
    pl.semaphore_wait(barrier, shards - 1)
    send_date(0)

    @pl.loop(1, dates)
    def _(date):
        compress(date)
        send_date(date)

    turned[...] = phase_ref[...].T

    @pl.loop(0, shards)
    def _(k):
        phase = turned[pl.ds(k, lanes, stride=shards), :].T
        at = pl.ds(pl.multiple_of(k * gates, gates), gates)
        trig[0, at, :] = jnp.cos(phase)
        trig[1, at, :] = jnp.sin(phase)

    for load in loads[:6]:
        load.wait()
    chunk = min(gates, 8)

    @pl.loop(0, dates)
    def _(date):
        arrived(date).wait_recv()
        for start in range(0, gates, chunk):
            part = pl.ds(start, chunk)
            re = [columns[date, s, 0, part, :].astype(jnp.float32) for s in range(shards)]
            im = [columns[date, s, 1, part, :].astype(jnp.float32) for s in range(shards)]
            re, im = fft_leading(re, im, -1.0)
            for k in range(shards):
                c, s = twid_ref[0, pl.ds(k, 1), :], twid_ref[1, pl.ds(k, 1), :]
                at = pl.ds(k * gates + start, chunk)
                work[at, :lanes] = re[k] * c + im[k] * s
                work[at, lanes:] = im[k] * c - re[k] * s
        spectrum = mm(work[...].astype(jnp.bfloat16), fwd_ref[...])
        c, s = trig[0], trig[1]
        re, im = spectrum[:, :lanes], spectrum[:, lanes:]
        shifted = jnp.concatenate([re * c - im * s, re * s + im * c], axis=1)
        work[...] = mm(shifted.astype(jnp.bfloat16), back_ref[...])
        for start in range(0, gates, chunk):
            re, im = [], []
            for k in range(shards):
                c, s = twid_ref[0, pl.ds(k, 1), :], twid_ref[1, pl.ds(k, 1), :]
                at = pl.ds(k * gates + start, chunk)
                a, b = work[at, :lanes], work[at, lanes:]
                re.append(a * c - b * s)
                im.append(b * c + a * s)
            re, im = fft_leading(re, im, 1.0)
            for n in range(shards):
                at = pl.ds(n * gates + start, chunk)
                focused[date, at, :lanes] = re[n].astype(jnp.bfloat16).astype(jnp.float32)
                focused[date, at, lanes:] = im[n].astype(jnp.bfloat16).astype(jnp.float32)

    looks_rows = gate_ref.shape[0] // 3
    gate_looks = looks_rows // shards

    def gathered(pair):
        part = pl.ds(0, shards - 1)
        return block(looks_sent.at[pair, part], looks_got.at[pair, part], dates + pair, ring(1))

    for pair in range(dates // 2):
        pieces, rim = [], None
        for d in (2 * pair, 2 * pair + 1):
            partner = lax.rem(d + offset_ref[d], dates)
            a, b = focused[d, :, :lanes], focused[d, :, lanes:]
            p, q = focused[partner, :, :lanes], focused[partner, :, lanes:]
            joined = jnp.concatenate([a * p + b * q, b * p - a * q], axis=1).astype(jnp.bfloat16)
            summed = mm(gate_ref[...], joined).astype(jnp.bfloat16)
            pieces.append(mm(summed[:looks_rows], main_ref[...]))
            sides = jnp.concatenate([summed[looks_rows : 2 * looks_rows], summed[2 * looks_rows :]], axis=1)
            side = mm(sides, rim_ref[d % 2])
            rim = side if rim is None else rim + side
        shaped = [piece.reshape(shards, gate_looks, lanes) for piece in pieces + [rim]]
        looks_sent[pair] = jnp.concatenate(shaped, axis=1).astype(looks_sent.dtype)

        @pl.loop(1, shards)
        def _(step):
            peer = ring(step)
            block(looks_sent.at[pair, peer], looks_got.at[pair, me], dates + pair, peer).start()

        looks_got[pair, me] = looks_sent[pair, me]

    for load in loads[6:]:
        load.wait()

    @pl.loop(0, dates)
    def _(date):
        arrived(date).wait_send()

    for pair in range(dates // 2):
        gathered(pair).wait_recv()
        received = looks_got[pair].astype(jnp.float32)

        def slab(index):
            return received[:, index * gate_looks : (index + 1) * gate_looks].reshape(shards * gate_looks, lanes)

        for parity in range(2):
            cells = jnp.concatenate([slab(parity), slab(2)], axis=1).astype(jnp.bfloat16)
            filter_date(cells, parity, 2 * pair + parity, *tables[6:], out_ref)

    for pair in range(dates // 2):
        gathered(pair).wait_send()


def focus_tables(shards, gates, lanes):
    total = shards * lanes
    k1, n2 = np.arange(shards), np.arange(lanes)
    angle = 2.0 * np.pi / total * (np.outer(k1, n2) % total)
    twiddle = np.stack([np.cos(angle), np.sin(angle)]).astype(np.float32)
    grid = np.exp(-2j * np.pi / lanes * (np.outer(n2, n2) % lanes))
    forward = right_block(grid)
    backward = right_block(np.conj(grid)) / total
    group = np.kron(np.eye(gates // ML_RG), np.ones((1, ML_RG)))
    before = np.eye(shards, k=-1)
    after = np.eye(shards, k=1)
    gate_sum = np.concatenate([np.kron(m, group) for m in (np.eye(shards), before, after)])
    looks = lanes // ML_AZ
    pair = np.kron(np.eye(looks), np.ones((ML_AZ, 1))) / (ML_RG * ML_AZ)
    main = np.kron(np.eye(2), pair)
    rim = np.zeros((2, 4 * lanes, lanes))
    for parity in range(2):
        for part in range(2):
            low = parity * 4 * HALF + part * 2 * HALF
            source = part * lanes
            rim[parity, source : source + lanes, low : low + HALF] = pair[:, looks - HALF :]
            source += 2 * lanes
            rim[parity, source : source + lanes, low + HALF : low + 2 * HALF] = pair[:, :HALF]
    bf16 = ml_dtypes.bfloat16
    return twiddle, forward.astype(bf16), backward.astype(bf16), gate_sum.astype(bf16), main.astype(bf16), rim.astype(bf16)


def filtered_looks(raw_echo, range_filter, azimuth_phase, pair_offset, shards):
    dates, _, lanes, total_gates = raw_echo.shape
    gates = azimuth_phase.shape[0]
    tables = focus_tables(shards, gates, lanes) + filter_tables(total_gates // ML_RG, lanes // ML_AZ)
    rows = shards * gates
    pairs = dates // 2
    block = (pairs, shards, 3 * (gates // ML_RG), lanes)
    columns = (dates, shards, 2, gates, lanes)
    return pl.pallas_call(
        functools.partial(stack_kernel, shards),
        in_specs=[pl.BlockSpec(memory_space=pltpu.SMEM)]
        + [VMEM] * 3
        + [pl.BlockSpec(memory_space=pl.ANY)] * len(tables),
        out_specs=VMEM,
        out_shape=jax.ShapeDtypeStruct((dates, 2, lanes // ML_AZ, total_gates // ML_RG), jnp.float32),
        scratch_shapes=[pltpu.VMEM(table.shape, table.dtype) for table in tables]
        + [
            pltpu.VMEM(columns, jnp.bfloat16),
            pltpu.VMEM(columns, jnp.bfloat16),
            pltpu.VMEM(azimuth_phase.shape[::-1], jnp.float32),
            pltpu.VMEM((2, rows, lanes), jnp.float32),
            pltpu.VMEM((rows, 2 * lanes), jnp.float32),
            pltpu.VMEM((dates, rows, 2 * lanes), jnp.float32),
            pltpu.VMEM(block, jnp.bfloat16),
            pltpu.VMEM(block, jnp.bfloat16),
            pltpu.SemaphoreType.DMA((dates + pairs,)),
            pltpu.SemaphoreType.DMA((dates + pairs,)),
            pltpu.SemaphoreType.DMA((len(tables),)),
        ],
        compiler_params=pltpu.CompilerParams(collective_id=0, has_side_effects=True),
        name="stack",
    )(pair_offset, raw_echo, range_filter, azimuth_phase, *tables)


def tri_window():
    return 1.0 - np.abs(np.arange(PATCH) - (PATCH - 1) / 2.0) / HALF


def patch_maps(cells, starts):
    count = len(starts)
    forward = np.zeros((cells, count, PATCH), np.complex128)
    backward = np.zeros((count, PATCH, cells), np.complex128)
    window, k = tri_window(), np.arange(PATCH)
    for patch, start in enumerate(starts):
        for a in range(PATCH):
            cell = start + a
            if 0 <= cell < cells:
                wave = np.exp(2j * np.pi / PATCH * (k * a % PATCH))
                forward[cell, patch] = np.conj(wave)
                backward[patch, :, cell] = wave * window[a] / PATCH
    return forward.reshape(cells, -1), backward.reshape(-1, cells)


def filter_tables(gate_rows, looks):
    gate_starts = range(-HALF, gate_rows - HALF + 1, HALF)
    line_starts = range(0, looks + 1, HALF)
    gate_fwd, gate_back = patch_maps(gate_rows, gate_starts)
    line_fwd, _ = patch_maps(looks + PATCH, line_starts)
    _, line_back = patch_maps(looks, [start - HALF for start in line_starts])
    used = len(line_starts) * PATCH
    width = -(-used // LANES) * LANES
    line_fwd = np.pad(line_fwd, ((0, 0), (0, width - used)))
    line_back = np.pad(line_back, ((0, width - used), (0, 0)))
    block = right_block(line_fwd).reshape(2, looks + PATCH, 2 * width)
    enter = np.zeros((2, 4 * looks, 2 * width))
    for parity in range(2):
        for part in range(2):
            enter[parity, part * looks : (part + 1) * looks] = block[part, HALF : HALF + looks]
            low = 2 * looks + parity * 4 * HALF + part * 2 * HALF
            enter[parity, low : low + HALF] = block[part, :HALF]
            enter[parity, low + HALF : low + 2 * HALF] = block[part, HALF + looks :]
    gap = (np.arange(PATCH)[:, None] - np.arange(PATCH)[None, :]) % PATCH
    near = (gap <= 1) | (gap == PATCH - 1)
    bf16 = ml_dtypes.bfloat16
    near_gate = np.kron(np.eye(len(gate_starts)), near).astype(bf16)
    near_line = np.kron(np.eye(width // PATCH), near).astype(bf16)
    level = np.kron(np.eye(width // PATCH), np.ones((PATCH, PATCH)) / PATCH**2).astype(bf16)
    return (
        enter.astype(bf16),
        left_block(gate_fwd.T).astype(bf16),
        near_gate,
        near_line,
        level,
        left_block(gate_back.T).astype(bf16),
        right_block(line_back).T.astype(bf16),
    )


def body(raw_echo, range_filter, azimuth_phase, pair_offset):
    shards = lax.axis_size("lines")
    image = filtered_looks(raw_echo, range_filter, azimuth_phase, pair_offset, shards)
    return image.transpose(0, 1, 3, 2)


def solution(mesh):
    placed = (P("groups", None, "lines", None), P(), P("lines", None), P())
    return jax.shard_map(
        body,
        mesh=mesh,
        in_specs=placed,
        out_specs=P("groups", None, None, "lines"),
        check_vma=False,
    )
```
